32 devices in a mesh: pgrp: 4 (over y, core), srow: 8 (over z, x).
Axes of the slice: x: 2, y: 2, z: 4, core: 2. Of those that a mesh axis runs over, the one named last changes fastest.
Arguments:
- kernel: bfloat16 [608, 224, 512], P('srow', None, 'pgrp'), may hold values from -0.0234375 to 0.0234375
- probes: bfloat16 [4, 608, 224], P(None, 'srow', 'pgrp'), may hold values from -6 to 6
- prior_var: float32 [512], P('pgrp'), may hold values from 0.3 to 3
- noise_var: float32 [608], P('srow'), may hold values from 0.1 to 1
Outputs:
- hessian_probes: float32 [4, 608, 224], P(None, 'srow', 'pgrp')
The draws below stay inside these ranges and needn't reach their ends.
All inputs are finite; a program needn't handle non-finite values.
Results may differ from the reference program's by a relative error of at most 0.0022.
Values may be sent and summed in bfloat16 or wider, within the bound.
No kernel may reach another device: no remote copies, remote signals or barrier semaphores. Data moves between devices by JAX's collectives and lax.ppermute only.
A program may use at most 64 MiB of HBM per device.

```python
import math
import jax
import jax.numpy as jnp
from jax import lax

NS = 608
NP = 512
NT = 224
NV = 4
N_SROW = 8


def block_scale(key, extent, cuts, least, high):
    gain = 1.0
    for axis_at, parts in cuts:
        heights = jax.random.uniform(jax.random.fold_in(jax.random.fold_in(key, 6), axis_at), (parts,), jnp.float32, least / len(cuts), high / len(cuts))
        gain = gain * jnp.repeat(jnp.exp(heights), extent[axis_at] // parts).reshape((-1,) + (1,) * (len(extent) - 1 - axis_at))
    return gain


def gaussian(key, dims, width, reach, shards=(), held_as=jnp.bfloat16):
    result = jax.random.normal(key, dims, jnp.float32) * width
    if len(shards) > 0:
        result = block_scale(key, dims, shards, -0.22, 0.18) * result
    return jnp.clip(result, min=-reach, max=reach).astype(held_as)


def setup_inputs(seed: int = 0) -> dict:
    arg_keys = jax.random.split(jax.random.key(seed), 5)
    return {
        "kernel": gaussian(arg_keys[0], (NS, NT, NP), (NT * (NS + NP) // 4) ** -0.5, 0.0234375, ((0, 8), (2, 4))),
        "probes": gaussian(arg_keys[1], (NV, NS, NT), 1.0, 6.0, ((1, 8), (2, 4))),
        "prior_var": jnp.clip(jnp.exp(math.log(3.0) - 2.3025851 * jax.random.uniform(arg_keys[2], (NP,), jnp.float32) ** block_scale(arg_keys[2], (NP,), ((0, 4),), -0.2, 0.2)), 0.3, 3.0),
        "noise_var": jnp.clip(jnp.exp(math.log(1.0) - 2.3025851 * jax.random.uniform(arg_keys[3], (NS,), jnp.float32) ** block_scale(arg_keys[3], (NS,), ((0, 8),), -0.2, 0.2)), 0.1, 1.0),
    }


def reference(kernel, probes, prior_var, noise_var):
    length = kernel.shape[1]
    padded_len = 2 * length
    per_block = NS // N_SROW
    probe_freq = jnp.fft.rfft(probes.astype(jnp.float32), n=padded_len, axis=2)
    freqs = probe_freq.shape[2]
    kernel_blocks = kernel.reshape(N_SROW, per_block, length, NP)
    probe_blocks = probe_freq.reshape(NV, N_SROW, per_block, freqs).transpose(1, 0, 2, 3)

    def adjoint_step(accum, pieces):
        kernel_piece, probe_piece = pieces
        kernel_freq = jnp.fft.rfft(kernel_piece.astype(jnp.float32), n=padded_len, axis=1)
        return accum + jnp.einsum('sfp,nsf->npf', jnp.conj(kernel_freq), probe_piece), None

    start = jnp.zeros((NV, NP, freqs), probe_freq.dtype)
    accum, unused = lax.scan(adjoint_step, start, (kernel_blocks, probe_blocks))
    adjoint = jnp.fft.irfft(accum, n=padded_len, axis=2)[:, :, :length]
    params = (adjoint * prior_var[None, :, None]).astype(jnp.bfloat16)
    param_freq = jnp.fft.rfft(params.astype(jnp.float32), n=padded_len, axis=2)

    def forward_step(kernel_piece):
        kernel_freq = jnp.fft.rfft(kernel_piece.astype(jnp.float32), n=padded_len, axis=1)
        product = jnp.einsum('sfp,npf->nsf', kernel_freq, param_freq)
        return jnp.fft.irfft(product, n=padded_len, axis=2)[:, :, :length]

    pieces = lax.map(forward_step, kernel_blocks)
    forward = pieces.transpose(1, 0, 2, 3).reshape(NV, NS, length)
    return forward + noise_var[None, :, None] * probes.astype(jnp.float32)
```

```python
import functools

import jax
import jax.numpy as jnp
from jax import lax
from jax.experimental import pallas as pl
from jax.experimental.pallas import tpu as pltpu
from jax.sharding import PartitionSpec as P

LAG = 16
STEP = 2 * LAG
SENSORS = 8
F32 = jnp.float32
BF16 = jnp.bfloat16


def chunk_rows(rows, parts):
    return -(-rows // (parts * LAG)) * LAG


def start_kernel_copy(kernel_hbm, kernel_vmem, sems, piece):
    copies = []
    sensors = kernel_hbm.shape[0]
    for at, first in enumerate(range(0, sensors, piece)):
        size = min(piece, sensors - first)
        span = pl.ds(first, size)
        copy = pltpu.make_async_copy(kernel_hbm.at[span], kernel_vmem.at[span], sems.at[at])
        copy.start()
        copies.append(copy)
    return copies


def adjoint_body(
    kernel_hbm, own, from1, from2, from3, out, kernel, slices, series, lhs, total, sems, *, scale
):
    sensors, length, width = kernel.shape
    probes, part = own.shape[0], own.shape[2]
    blocks = length // STEP
    rows = probes * STEP
    piece = 2 * SENSORS
    copies = start_kernel_copy(kernel_hbm, kernel, sems, piece)
    me = lax.axis_index("pgrp")
    for offset, held in enumerate((own, from1, from2, from3)):
        slices[me ^ offset] = held[...]
    series[...] = jnp.zeros_like(series)
    for at in range(length // part):
        value = slices[at].astype(F32)
        for side in range(2):
            first = max(at * part, side * 128)
            last = min((at + 1) * part, (side + 1) * 128)
            if first < last:
                series[side, :, :sensors, first - side * 128 : last - side * 128] = value[
                    :, :, first - at * part : last - at * part
                ]
    lane = lax.broadcasted_iota(jnp.int32, (SENSORS, 128), 1)
    sub = lax.broadcasted_iota(jnp.int32, (SENSORS, 128), 0)
    groups = -(-sensors // SENSORS)
    for group in range(2 * -(-groups // 2)):
        count = max(0, min(SENSORS, sensors - group * SENSORS))
        for n in range(probes):
            low, high = [], []
            for s in range(group * SENSORS, group * SENSORS + count):
                first = series[0, n, pl.ds(s, 8, stride=0), :]
                second = series[1, n, pl.ds(s, 8, stride=0), :]
                for half in range(2):
                    shift = sub + 8 * half
                    index = (lane + shift) % 128
                    one = jnp.take_along_axis(first, index, axis=1, mode="promise_in_bounds")
                    two = jnp.take_along_axis(second, index, axis=1, mode="promise_in_bounds")
                    low.append(jnp.where(lane + shift < 128, one, two))
                    high.append(two)
            fill = [jnp.zeros((8, 128), F32)] * (2 * (SENSORS - count))
            for at, parts in enumerate((low, high)):
                turned = jnp.concatenate(parts + fill, axis=0).T.astype(BF16)
                for o in range(4 * at, min(4 * at + 4, blocks)):
                    first_row = (o - 4 * at) * STEP
                    lhs[group, o * rows + n * STEP : o * rows + (n + 1) * STEP, :] = turned[
                        first_row : first_row + STEP
                    ]
    for copy in copies:
        copy.wait()
    for j in range(blocks):
        acc = None
        for c in range(-(-sensors // piece)):
            count = min(piece, sensors - c * piece)
            span = slice(c * piece, c * piece + count)
            sides = []
            for e in range(2):
                lags = slice(STEP * j + LAG * e, STEP * j + LAG * (e + 1))
                side = kernel[span, lags, :].reshape(count * LAG, width)
                if count < piece:
                    side = jnp.concatenate(
                        [side, jnp.zeros(((piece - count) * LAG, width), BF16)], axis=0
                    )
                sides.append(side)
            right = jnp.concatenate(sides, axis=1)
            left = jnp.concatenate(
                [lhs[2 * c, j * rows :, :], lhs[2 * c + 1, j * rows :, :]], axis=1
            )
            product = jnp.dot(left, right, preferred_element_type=F32)
            acc = product if acc is None else acc + product
        span = slice(0, (blocks - j) * rows)
        if j == 0:
            total[...] = acc
        else:
            total[span, :] += acc
    if out.shape[0] > blocks * rows:
        out[blocks * rows :, :] = jnp.zeros((out.shape[0] - blocks * rows, width), F32)
    for o in range(blocks):
        for n in range(probes):
            for t in range(0, STEP, 8):
                at = o * rows + n * STEP + t
                value = total[at : at + 8, :width]
                if t < LAG:
                    value = value + total[at + LAG : at + LAG + 8, width:]
                elif o + 1 < blocks:
                    at = at + rows - LAG
                    value = value + total[at : at + 8, width:]
                out[pl.ds(o * rows + t * probes + n, 8, stride=probes), :] = value * scale


def adjoint(kernel, held, padded_rows, scale):
    sensors, length, width = kernel.shape
    probes, part = held[0].shape[0], held[0].shape[2]
    groups = 2 * -(-sensors // (2 * SENSORS))
    rows = probes * length
    return pl.pallas_call(
        functools.partial(adjoint_body, scale=scale),
        out_shape=jax.ShapeDtypeStruct((padded_rows, width), F32),
        in_specs=[pl.BlockSpec(memory_space=pl.ANY)]
        + [pl.BlockSpec(memory_space=pltpu.VMEM)] * len(held),
        out_specs=pl.BlockSpec(memory_space=pltpu.VMEM),
        scratch_shapes=[
            pltpu.VMEM(kernel.shape, BF16),
            pltpu.VMEM((length // part,) + held[0].shape, BF16),
            pltpu.VMEM((2, probes, -(-sensors // 8) * 8, 128), F32),
            pltpu.VMEM((groups, rows, 128), BF16),
            pltpu.VMEM((rows, 2 * width), F32),
            pltpu.SemaphoreType.DMA((groups // 2,)),
        ],
        name="adjoint",
    )(kernel, *held)


def merge(first, second, step, sub):
    mine = (sub & step) == 0
    return jnp.where(mine, first, second) + pltpu.roll(jnp.where(mine, second, first), step, 0)


def forward_body(
    kernel_hbm, params, own, to1, to2, to3, kernel, weights, product, held, result, sums, sems
):
    sensors, length, width = kernel.shape
    blocks = length // STEP
    rows = weights.shape[1]
    half = rows // 2
    probes = rows // STEP
    copies = start_kernel_copy(kernel_hbm, kernel, sems, 2 * SENSORS)
    for d in range(blocks):
        weights[d, :, :width] = params[d * rows : (d + 1) * rows, :]
        weights[d, half:, width:] = params[d * rows : d * rows + half, :]
        if d == 0:
            weights[d, :half, width:] = jnp.zeros((half, width), BF16)
        else:
            weights[d, :half, width:] = params[d * rows - half : d * rows, :]
    for copy in copies:
        copy.wait()
    lane = lax.broadcasted_iota(jnp.int32, (8, 128), 1)
    sub = lax.broadcasted_iota(jnp.int32, (8, 128), 0)
    sets = [(o - 1, o) for o in range(blocks - 1, 0, -2)][::-1]
    if blocks % 2:
        sets = [(0,)] + sets
    for members in sets:
        acc = None
        for j in range(members[-1] + 1):
            left = jnp.concatenate(
                [
                    kernel[:, STEP * j + LAG * e : STEP * j + LAG * (e + 1), :].reshape(
                        sensors * LAG, width
                    )
                    for e in range(2)
                ],
                axis=1,
            )
            right = jnp.concatenate(
                [
                    weights[o - j] if o >= j else jnp.zeros((rows, 2 * width), BF16)
                    for o in members
                ],
                axis=0,
            )
            part = lax.dot_general(
                left, right, (((1,), (1,)), ((), ())), preferred_element_type=F32
            )
            acc = part if acc is None else acc + part
        product[:, : len(members) * rows] = acc
        for at, o in enumerate(members):
            for group in range(-(-sensors // SENSORS)):
                summed = []
                for s in range(group * SENSORS, (group + 1) * SENSORS):
                    if s >= sensors:
                        summed.append(jnp.zeros((8, 128), F32))
                        continue
                    value = None
                    for h in range(2):
                        first = s * LAG + 8 * h
                        turned = pltpu.roll(
                            product[first : first + 8, at * rows : (at + 1) * rows],
                            8 * h * probes,
                            1,
                            stride=probes,
                            stride_axis=0,
                        )
                        inside = lane >= (sub + 8 * h) * probes
                        before = held[first : first + 8, :] if o > 0 else jnp.zeros_like(turned)
                        mixed = jnp.where(inside, turned, before)
                        if o + 1 < blocks:
                            held[first : first + 8, :] = turned
                        value = mixed if value is None else value + mixed
                    summed.append(value)
                step = 1
                while len(summed) > 1:
                    summed = [
                        merge(summed[k], summed[k + 1], step, sub)
                        for k in range(0, len(summed), 2)
                    ]
                    step *= 2
                result[group * SENSORS : (group + 1) * SENSORS, o * rows : (o + 1) * rows] = (
                    summed[0]
                )
    span = own.shape[1]
    for q in range(sums.shape[0]):
        sums[q] = result[:sensors, q * span : (q + 1) * span]
    me = lax.axis_index("pgrp")
    own[...] = sums[me]
    for offset, to in enumerate((to1, to2, to3)):
        to[...] = sums[me ^ (offset + 1)].astype(BF16)


def forward(params, kernel, probes, parts):
    sensors, length, width = kernel.shape
    rows = probes * STEP
    span = probes * length // parts
    groups = -(-sensors // (2 * SENSORS))
    padded = -(-sensors // SENSORS) * SENSORS
    return pl.pallas_call(
        forward_body,
        out_shape=[jax.ShapeDtypeStruct((sensors, span), F32)]
        + [jax.ShapeDtypeStruct((sensors, span), BF16)] * (parts - 1),
        in_specs=[
            pl.BlockSpec(memory_space=pl.ANY),
            pl.BlockSpec(memory_space=pltpu.VMEM),
        ],
        out_specs=[pl.BlockSpec(memory_space=pltpu.VMEM)] * parts,
        scratch_shapes=[
            pltpu.VMEM(kernel.shape, BF16),
            pltpu.VMEM((length // STEP, rows, 2 * width), BF16),
            pltpu.VMEM((sensors * LAG, 2 * rows), F32),
            pltpu.VMEM((sensors * LAG, rows), F32),
            pltpu.VMEM((padded, probes * length), F32),
            pltpu.VMEM((parts, sensors, span), F32),
            pltpu.SemaphoreType.DMA((groups,)),
        ],
        name="forward",
    )(kernel, params)


def finish_body(own, from1, from2, from3, probes, noise, out):
    count, sensors, part = out.shape
    total = own[...] + from1[...].astype(F32) + from2[...].astype(F32) + from3[...].astype(F32)
    span = total.shape[1]
    lane = lax.broadcasted_iota(jnp.int32, (sensors, 128), 1)
    pieces = []
    for first in range(0, span, 128):
        piece = total[:, first : first + 128]
        if piece.shape[1] < 128:
            piece = jnp.concatenate(
                [piece, jnp.zeros((sensors, 128 - piece.shape[1]), F32)], axis=1
            )
        pieces.append(piece)
    scale = jnp.broadcast_to(
        jnp.concatenate([noise[...], jnp.zeros((1, 128 - sensors), F32)], axis=1), (128, 128)
    ).T[:sensors, :]
    per = 128 // count
    for n in range(count):
        index = (count * lane + n) % 128
        value = None
        for at, piece in enumerate(pieces):
            got = jnp.take_along_axis(piece, index, axis=1, mode="promise_in_bounds")
            value = got if value is None else jnp.where(lane < at * per, value, got)
        out[n] = value[:, :part] + scale[:, :part] * probes[n].astype(F32)


def finish(own, others, probes, noise):
    count, sensors, part = probes.shape
    return pl.pallas_call(
        finish_body,
        out_shape=jax.ShapeDtypeStruct(probes.shape, F32),
        name="finish",
    )(own, *others, probes, noise.reshape(1, sensors))


def swaps(array_of, parts):
    return [
        lax.ppermute(array_of(offset), "pgrp", [(i, i ^ offset) for i in range(parts)])
        for offset in range(1, parts)
    ]


def on_device(kernel, probes, prior_var, noise_var, *, parts, peers):
    sensors, length, width = kernel.shape
    count = probes.shape[0]
    rows = count * length
    chunk = chunk_rows(rows, peers)
    held = [probes] + swaps(lambda offset: probes, parts)
    partial = adjoint(kernel, held, chunk * peers, 16.0)
    sent = partial.reshape(peers, chunk, width).astype(jnp.float16)
    got = lax.all_to_all(sent, "srow", 0, 0, tiled=True)
    totals = jnp.sum(got.astype(F32), axis=0) * (1.0 / 16.0)
    params = (totals * prior_var[None, :]).astype(BF16)
    params = jnp.broadcast_to(params[None], (peers, chunk, width))
    params = lax.all_to_all(params, "srow", 0, 0, tiled=True).reshape(peers * chunk, width)
    shares = forward(params, kernel, count, parts)
    others = swaps(lambda offset: shares[offset], parts)
    return finish(shares[0], others, probes, noise_var)


def solution(mesh):
    placed = (P("srow", None, "pgrp"), P(None, "srow", "pgrp"), P("pgrp"), P("srow"))
    body = functools.partial(
        on_device, parts=mesh.shape["pgrp"], peers=mesh.shape["srow"]
    )
    return jax.shard_map(
        body, mesh=mesh, in_specs=placed, out_specs=P(None, "srow", "pgrp"), check_vma=False
    )
```

```python
import functools

import jax
import jax.numpy as jnp
from jax import lax
from jax.experimental import pallas as pl
from jax.experimental.pallas import tpu as pltpu
from jax.sharding import PartitionSpec as P

LAG = 16
STEP = 2 * LAG
SENSORS = 8
F32 = jnp.float32
BF16 = jnp.bfloat16


def in_vmem(array):
    return pltpu.with_memory_space_constraint(array, pltpu.VMEM)


def causal_sets(blocks):
    sets = [(o - 1, o) for o in range(blocks - 1, 0, -2)][::-1]
    return [(0,)] + sets if blocks % 2 else sets


def sensor_groups(sensors):
    return [
        (first, min(first + SENSORS, sensors)) for first in range(0, sensors, SENSORS)
    ]


def prepare_body(kernel_hbm, own_hbm, prior, kernel, turned, own, variance, sems):
    sensors, length, width = kernel.shape
    groups = sensor_groups(sensors)
    copies = [pltpu.make_async_copy(own_hbm, own, sems.at[len(groups)])]
    for at, (first, last) in enumerate(groups):
        span = pl.ds(first, last - first)
        copies.append(pltpu.make_async_copy(kernel_hbm.at[span], kernel.at[span], sems.at[at]))
    for copy in copies:
        copy.start()
    variance[...] = jnp.broadcast_to(prior[...], (width, width)).T
    copies[0].wait()
    for at, (first, last) in enumerate(groups):
        copies[1 + at].wait()
        for a in range(length // LAG):
            tile = kernel[first:last, a * LAG : (a + 1) * LAG, :].reshape(-1, width)
            if last - first < SENSORS:
                fill = jnp.zeros(((SENSORS - last + first) * LAG, width), BF16)
                tile = jnp.concatenate([tile, fill], axis=0)
            turned[a * width : (a + 1) * width, at * 128 : (at + 1) * 128] = tile.T
    spare = turned.shape[1] - len(groups) * 128
    if spare:
        turned[:, len(groups) * 128 :] = jnp.zeros((turned.shape[0], spare), BF16)


def prepare(kernel, series, prior_var):
    sensors, length, width = kernel.shape
    lanes = 256 * -(-sensors // (2 * SENSORS))
    vmem = pl.BlockSpec(memory_space=pltpu.VMEM)
    hbm = pl.BlockSpec(memory_space=pltpu.HBM)
    return pl.pallas_call(
        prepare_body,
        out_shape=[
            pltpu.VMEM(kernel.shape, BF16),
            pltpu.VMEM((length // LAG * width, lanes), BF16),
            pltpu.VMEM(series.shape, BF16),
            pltpu.VMEM((width, width), F32),
        ],
        in_specs=[hbm, hbm, vmem],
        out_specs=[vmem] * 4,
        scratch_shapes=[pltpu.SemaphoreType.DMA((len(sensor_groups(sensors)) + 1,))],
        compiler_params=pltpu.CompilerParams(vmem_limit_bytes=105 << 19),
        name="prepare",
    )(kernel, series, prior_var.reshape(1, width))


def adjoint_body(
    turned,
    variance,
    own,
    from1,
    from2,
    from3,
    resident,
    out,
    kept,
    tall,
    series,
    right,
    product,
    even,
    odd,
):
    width = variance.shape[0]
    probes, part, sensors = own.shape
    rows = probes * STEP
    blocks = tall.shape[0] // rows
    me = lax.axis_index("pgrp")
    for offset, held in enumerate((own, from1, from2, from3)):
        first = (me ^ offset) * (part * probes)
        for n in range(probes):
            tall[pl.ds(first + n, part, stride=probes), :sensors] = held[n].astype(F32)
    for o in range(blocks):
        series[o] = tall[o * rows : (o + 1) * rows, :].astype(BF16).T.astype(F32)
    lane = lax.broadcasted_iota(jnp.int32, (8, 128), 1)
    sub = lax.broadcasted_iota(jnp.int32, (8, 128), 0)
    sets = causal_sets(blocks)
    padded = right.shape[0] // LAG
    if padded > sensors:
        right[sensors * LAG :, :] = jnp.zeros(((padded - sensors) * LAG, right.shape[1]), BF16)

    def expand(s, first, last):
        tiles = {}
        for half in range(2):
            shift = (sub + 8 * half) * probes
            index = (lane + shift) % 128
            inside = lane + shift < 128
            held = None
            for o in range(first, min(last + 2, blocks)):
                row = series[o, pl.ds(s, 8, stride=0), :]
                moved = jnp.take_along_axis(row, index, axis=1, mode="promise_in_bounds")
                if held is not None:
                    tiles[o - 1, half] = jnp.where(inside, held, moved)
                held = moved
            if last + 1 == blocks:
                tiles[last, half] = jnp.where(inside, held, 0.0)
        for o in range(first, last + 1):
            right[s * LAG : (s + 1) * LAG, o * rows : (o + 1) * rows] = jnp.concatenate(
                [tiles[o, 0], tiles[o, 1]], axis=0
            ).astype(BF16)

    def multiply(members):
        tall_rows = (members[-1] + 1) * 2 * width
        columns = slice(members[0] * rows, (members[-1] + 1) * rows)
        pieces = -(-tall_rows // 512)
        piece = -(-tall_rows // (pieces * 128)) * 128
        for first in range(0, tall_rows, piece):
            last = min(first + piece, tall_rows)
            acc = None
            for at in range(0, turned.shape[1], 256):
                step = jnp.dot(
                    turned[first:last, at : at + 256],
                    right[at : at + 256, columns],
                    preferred_element_type=F32,
                )
                acc = step if acc is None else acc + step
            product[first:last, : len(members) * rows] = acc

    def gather(members):
        for place, o in enumerate(members):
            for j in range(o + 1):
                for e, sums in enumerate((even, odd)):
                    at = (2 * j + e) * width
                    value = product[at : at + width, place * rows : (place + 1) * rows]
                    if j == 0:
                        sums[o] = value
                    else:
                        sums[o - j] += value

    for members in sets:
        for s in range(sensors):
            expand(s, members[0], members[-1])
        multiply(members)
        gather(members)

    most = jnp.zeros((8, rows), F32)
    first_half = lane < rows // 2
    scale = variance[...]
    for first in range(0, width, 8):
        span = slice(first, first + 8)
        after = None
        for o in range(blocks - 1, -1, -1):
            moved = pltpu.roll(odd[o, span, :], rows // 2, 1)
            late = jnp.where(first_half, moved, 0.0 if after is None else after)
            after = moved
            value = (even[o, span, :] + late) * scale[span, :]
            even[o, span, :] = value
            most = jnp.maximum(most, jnp.abs(value))
    peak = jnp.maximum(jnp.max(most, axis=(0, 1), keepdims=True), 2.0**-100)
    power = jnp.floor(jnp.log2(peak))
    gain = jnp.exp2(14.0 - jnp.broadcast_to(power, (width, rows)))
    for o in range(blocks):
        out[:, o * rows : (o + 1) * rows] = even[o] * gain
    out[:, blocks * rows :] = jnp.broadcast_to(power, (width, rows))


def adjoint(turned, variance, held, resident):
    width = variance.shape[0]
    probes, part, sensors = held[0].shape
    rows = probes * STEP
    blocks = turned.shape[0] // (2 * width)
    vmem = pl.BlockSpec(memory_space=pltpu.VMEM)
    return pl.pallas_call(
        adjoint_body,
        out_shape=[
            pltpu.VMEM((width, (blocks + 1) * rows), F32),
            pltpu.VMEM(resident.shape, BF16),
        ],
        in_specs=[vmem] * (3 + len(held)),
        out_specs=[vmem, vmem],
        input_output_aliases={2 + len(held): 1},
        scratch_shapes=[
            pltpu.VMEM((blocks * rows, 128), F32),
            pltpu.VMEM((blocks, 128, rows), F32),
            pltpu.VMEM((turned.shape[1], blocks * rows), BF16),
            pltpu.VMEM((blocks * 2 * width, 2 * rows), F32),
            pltpu.VMEM((blocks, width, rows), F32),
            pltpu.VMEM((blocks, width, rows), F32),
        ],
        compiler_params=pltpu.CompilerParams(vmem_limit_bytes=24 << 20),
        name="adjoint",
    )(turned, variance, *[in_vmem(array) for array in held], resident)


def decode_body(got, out):
    peers, own_rows, columns = out.shape
    total = None
    for r in range(peers):
        gain = jnp.exp2(got[r, :, columns : columns + 128] - 14.0)
        parts = [got[r, :, at : at + 128] * gain for at in range(0, columns, 128)]
        total = parts if total is None else [x + y for x, y in zip(total, parts)]
    for at, value in enumerate(total):
        for r in range(peers):
            out[r, :, at * 128 : (at + 1) * 128] = value.astype(BF16)


def decode(got, columns):
    vmem = pl.BlockSpec(memory_space=pltpu.VMEM)
    return pl.pallas_call(
        decode_body,
        out_shape=pltpu.VMEM(got.shape[:2] + (columns,), BF16),
        in_specs=[vmem],
        out_specs=vmem,
        compiler_params=pltpu.CompilerParams(vmem_limit_bytes=24 << 20),
        name="decode",
    )(in_vmem(got))


def merge(first, second, step, sub):
    mine = (sub & step) == 0
    return jnp.where(mine, first, second) + pltpu.roll(jnp.where(mine, second, first), step, 0)


def forward_body(kernel, params, own, to1, to2, to3, weights, product, held, result, tall):
    sensors, length, width = kernel.shape
    probes, part = own.shape[0], own.shape[1]
    blocks = length // STEP
    rows = weights.shape[2]
    half = rows // 2
    for d in range(blocks):
        here = params[:, d * rows : (d + 1) * rows]
        weights[d, :width, :] = here
        if d == 0:
            before = jnp.zeros((width, half), BF16)
        else:
            before = params[:, d * rows - half : d * rows]
        weights[d, width:, :] = jnp.concatenate([before, here[:, :half]], axis=1)
    lane = lax.broadcasted_iota(jnp.int32, (8, 128), 1)
    sub = lax.broadcasted_iota(jnp.int32, (8, 128), 0)
    sets = causal_sets(blocks)

    def multiply(at, first, last):
        members = sets[at]
        acc = None
        for j in range(members[-1] + 1):
            left = jnp.concatenate(
                [
                    kernel[first:last, STEP * j + LAG * e : STEP * j + LAG * (e + 1), :].reshape(
                        (last - first) * LAG, width
                    )
                    for e in range(2)
                ],
                axis=1,
            )
            right = jnp.concatenate(
                [
                    weights[o - j] if o >= j else jnp.zeros((2 * width, rows), BF16)
                    for o in members
                ],
                axis=1,
            )
            step = jnp.dot(left, right, preferred_element_type=F32)
            acc = step if acc is None else acc + step
        product[at, first * LAG : last * LAG, : len(members) * rows] = acc

    def skew(at, group):
        for place, o in enumerate(sets[at]):
            summed = []
            for s in range(group * SENSORS, (group + 1) * SENSORS):
                if s >= sensors:
                    summed.append(jnp.zeros((8, 128), F32))
                    continue
                value = None
                for h in range(2):
                    first = s * LAG + 8 * h
                    shifted = pltpu.roll(
                        product[at, first : first + 8, place * rows : (place + 1) * rows],
                        8 * h * probes,
                        1,
                        stride=probes,
                        stride_axis=0,
                    )
                    inside = lane >= (sub + 8 * h) * probes
                    before = held[first : first + 8, :] if o > 0 else jnp.zeros_like(shifted)
                    mixed = jnp.where(inside, shifted, before)
                    if o + 1 < blocks:
                        held[first : first + 8, :] = shifted
                    value = mixed if value is None else value + mixed
                summed.append(value)
            step = 1
            while len(summed) > 1:
                summed = [
                    merge(summed[k], summed[k + 1], step, sub) for k in range(0, len(summed), 2)
                ]
                step *= 2
            result[o, group * SENSORS : (group + 1) * SENSORS, :] = summed[0]

    groups = range(-(-sensors // SENSORS))
    pieces = -(-sensors // 40)
    piece = -(-len(groups) // pieces)
    for at in range(len(sets) + 1):
        for first in range(0, len(groups), piece):
            if at < len(sets):
                multiply(at, first * SENSORS, min((first + piece) * SENSORS, sensors))
            if at > 0:
                for group in groups[first : first + piece]:
                    skew(at - 1, group)
    for o in range(blocks):
        tall[o * rows : (o + 1) * rows, :] = result[o].T
    me = lax.axis_index("pgrp")
    for offset, to in enumerate((own, to1, to2, to3)):
        first = (me ^ offset) * (part * probes)
        for n in range(probes):
            share = tall[pl.ds(first + n, part, stride=probes), :]
            to[n] = share[:, :sensors].astype(to.dtype)


def forward(params, kernel, shape, parts):
    sensors, length, width = kernel.shape
    probes = shape[0]
    rows = probes * STEP
    blocks = length // STEP
    vmem = pl.BlockSpec(memory_space=pltpu.VMEM)
    return pl.pallas_call(
        forward_body,
        out_shape=[pltpu.VMEM(shape, F32)] + [pltpu.VMEM(shape, BF16)] * (parts - 1),
        in_specs=[vmem, vmem],
        out_specs=[vmem] * parts,
        scratch_shapes=[
            pltpu.VMEM((blocks, 2 * width, rows), BF16),
            pltpu.VMEM((blocks // 2 + 1, sensors * LAG, 2 * rows), F32),
            pltpu.VMEM((sensors * LAG, rows), F32),
            pltpu.VMEM((blocks, 128, rows), F32),
            pltpu.VMEM((blocks * rows, 128), F32),
        ],
        compiler_params=pltpu.CompilerParams(vmem_limit_bytes=24 << 20),
        name="forward",
    )(kernel, in_vmem(params))


def swaps(array_of, parts):
    return [
        lax.ppermute(array_of(offset), "pgrp", [(i, i ^ offset) for i in range(parts)])
        for offset in range(1, parts)
    ]


def on_device(kernel, probes, prior_var, noise_var, *, parts, peers):
    width = kernel.shape[2]
    series = probes.transpose(0, 2, 1)
    columns = series.shape[0] * kernel.shape[1]
    others = swaps(lambda offset: series, parts)
    resident, turned, own, variance = prepare(kernel, series, prior_var)
    partial, resident = adjoint(turned, variance, [own] + others, resident)
    sent = partial.astype(jnp.float16).reshape(peers, width // peers, -1)
    got = lax.all_to_all(sent, "srow", 0, 0, tiled=True).astype(F32)
    params = decode(got, columns)
    params = lax.all_to_all(params, "srow", 0, 0, tiled=True).reshape(width, columns)
    shares = forward(params, resident, series.shape, parts)
    total = shares[0]
    for other in swaps(lambda offset: shares[offset], parts):
        total = total + other.astype(F32)
    total = total + noise_var[None, None, :] * series.astype(F32)
    return total.transpose(0, 2, 1)


def solution(mesh):
    placed = (P("srow", None, "pgrp"), P(None, "srow", "pgrp"), P("pgrp"), P("srow"))
    body = functools.partial(
        on_device, parts=mesh.shape["pgrp"], peers=mesh.shape["srow"]
    )
    return jax.shard_map(
        body, mesh=mesh, in_specs=placed, out_specs=P(None, "srow", "pgrp"), check_vma=False
    )
```

```python
import functools

import jax
import jax.numpy as jnp
from jax import lax
from jax.experimental import pallas as pl
from jax.experimental.pallas import tpu as pltpu
from jax.sharding import PartitionSpec as P

LAG = 16
STEP = 2 * LAG
SENSORS = 8
NEAR = 4
TOP = 14.0
F32 = jnp.float32
BF16 = jnp.bfloat16


def in_vmem(array):
    return pltpu.with_memory_space_constraint(array, pltpu.VMEM)


def causal_sets(blocks):
    sets = [(o - 1, o) for o in range(blocks - 1, 0, -2)][::-1]
    return [(0,)] + sets if blocks % 2 else sets


def sensor_groups(sensors):
    return [
        (first, min(first + SENSORS, sensors)) for first in range(0, sensors, SENSORS)
    ]


def prepare_body(kernel_hbm, own_hbm, prior, kernel, turned, own, variance, sems):
    sensors, length, width = kernel.shape
    groups = sensor_groups(sensors)
    copies = [pltpu.make_async_copy(own_hbm, own, sems.at[len(groups)])]
    for at, (first, last) in enumerate(groups):
        span = pl.ds(first, last - first)
        copies.append(pltpu.make_async_copy(kernel_hbm.at[span], kernel.at[span], sems.at[at]))
    for copy in copies:
        copy.start()
    variance[...] = jnp.broadcast_to(prior[...], (width, width)).T
    copies[0].wait()
    for at, (first, last) in enumerate(groups):
        copies[1 + at].wait()
        for a in range(length // LAG):
            tile = kernel[first:last, a * LAG : (a + 1) * LAG, :].reshape(-1, width)
            if last - first < SENSORS:
                fill = jnp.zeros(((SENSORS - last + first) * LAG, width), BF16)
                tile = jnp.concatenate([tile, fill], axis=0)
            turned[a * width : (a + 1) * width, at * 128 : (at + 1) * 128] = tile.T
    spare = turned.shape[1] - len(groups) * 128
    if spare:
        turned[:, len(groups) * 128 :] = jnp.zeros((turned.shape[0], spare), BF16)


def prepare(kernel, series, prior_var):
    sensors, length, width = kernel.shape
    lanes = 256 * -(-sensors // (2 * SENSORS))
    vmem = pl.BlockSpec(memory_space=pltpu.VMEM)
    hbm = pl.BlockSpec(memory_space=pltpu.HBM)
    return pl.pallas_call(
        prepare_body,
        out_shape=[
            pltpu.VMEM(kernel.shape, BF16),
            pltpu.VMEM((length // LAG * width, lanes), BF16),
            pltpu.VMEM(series.shape, BF16),
            pltpu.VMEM((width, width), F32),
        ],
        in_specs=[hbm, hbm, vmem],
        out_specs=[vmem] * 4,
        scratch_shapes=[pltpu.SemaphoreType.DMA((len(sensor_groups(sensors)) + 1,))],
        compiler_params=pltpu.CompilerParams(vmem_limit_bytes=105 << 19),
        name="prepare",
    )(kernel, series, prior_var.reshape(1, width))


def scaling(most):
    peak = jnp.maximum(jnp.max(most, axis=(0, 1), keepdims=True), 2.0**-100)
    power = jnp.floor(jnp.log2(peak))
    return power, jnp.exp2(TOP - power)


def adjoint_body(
    turned,
    variance,
    own,
    from1,
    from2,
    from3,
    resident,
    mine,
    to1,
    to2,
    to3,
    kept,
    tall,
    series,
    right,
    product,
    even,
    odd,
):
    width = variance.shape[0]
    probes, part, sensors = own.shape
    rows = probes * STEP
    blocks = tall.shape[0] // rows
    me = lax.axis_index("pgrp")
    for offset, held in enumerate((own, from1, from2, from3)):
        first = (me ^ offset) * (part * probes)
        for n in range(probes):
            tall[pl.ds(first + n, part, stride=probes), :sensors] = held[n].astype(F32)
    for o in range(blocks):
        series[o] = tall[o * rows : (o + 1) * rows, :].astype(BF16).T.astype(F32)
    lane = lax.broadcasted_iota(jnp.int32, (8, 128), 1)
    sub = lax.broadcasted_iota(jnp.int32, (8, 128), 0)
    sets = causal_sets(blocks)
    padded = right.shape[0] // LAG
    if padded > sensors:
        right[sensors * LAG :, :] = jnp.zeros(((padded - sensors) * LAG, right.shape[1]), BF16)

    def expand(s, first, last):
        tiles = {}
        for half in range(2):
            shift = (sub + 8 * half) * probes
            index = (lane + shift) % 128
            inside = lane + shift < 128
            held = None
            for o in range(first, min(last + 2, blocks)):
                row = series[o, pl.ds(s, 8, stride=0), :]
                moved = jnp.take_along_axis(row, index, axis=1, mode="promise_in_bounds")
                if held is not None:
                    tiles[o - 1, half] = jnp.where(inside, held, moved)
                held = moved
            if last + 1 == blocks:
                tiles[last, half] = jnp.where(inside, held, 0.0)
        for o in range(first, last + 1):
            right[s * LAG : (s + 1) * LAG, o * rows : (o + 1) * rows] = jnp.concatenate(
                [tiles[o, 0], tiles[o, 1]], axis=0
            ).astype(BF16)

    def multiply(members):
        tall_rows = (members[-1] + 1) * 2 * width
        columns = slice(members[0] * rows, (members[-1] + 1) * rows)
        pieces = -(-tall_rows // 512)
        piece = -(-tall_rows // (pieces * 128)) * 128
        for first in range(0, tall_rows, piece):
            last = min(first + piece, tall_rows)
            acc = None
            for at in range(0, turned.shape[1], 256):
                step = jnp.dot(
                    turned[first:last, at : at + 256],
                    right[at : at + 256, columns],
                    preferred_element_type=F32,
                )
                acc = step if acc is None else acc + step
            product[first:last, : len(members) * rows] = acc

    def gather(members):
        for place, o in enumerate(members):
            for j in range(o + 1):
                for e, sums in enumerate((even, odd)):
                    at = (2 * j + e) * width
                    value = product[at : at + width, place * rows : (place + 1) * rows]
                    if j == 0:
                        sums[o] = value
                    else:
                        sums[o - j] += value

    for members in sets:
        for s in range(sensors):
            expand(s, members[0], members[-1])
        multiply(members)
        gather(members)

    most = jnp.zeros((8, rows), F32)
    first_half = lane < rows // 2
    scale = variance[...]
    for first in range(0, width, 8):
        span = slice(first, first + 8)
        after = None
        for o in range(blocks - 1, -1, -1):
            moved = pltpu.roll(odd[o, span, :], rows // 2, 1)
            late = jnp.where(first_half, moved, 0.0 if after is None else after)
            after = moved
            value = (even[o, span, :] + late) * scale[span, :]
            even[o, span, :] = value
            most = jnp.maximum(most, jnp.abs(value))
    power, gain = scaling(most)
    block = mine.shape[0]
    near = lax.axis_index("srow") % NEAR
    for o in range(blocks):
        columns = slice(o * rows, (o + 1) * rows)
        mine[:, columns] = even[o, pl.ds(near * block, block), :]
        for offset, to in enumerate((to1, to2, to3)):
            first = (near ^ (offset + 1)) * block
            to[:, columns] = even[o, pl.ds(first, block), :] * gain
    for to in (to1, to2, to3):
        to[:, blocks * rows :] = jnp.broadcast_to(power, (block, rows))


def adjoint(turned, variance, held, resident):
    width = variance.shape[0]
    probes, part, sensors = held[0].shape
    rows = probes * STEP
    blocks = turned.shape[0] // (2 * width)
    vmem = pl.BlockSpec(memory_space=pltpu.VMEM)
    return pl.pallas_call(
        adjoint_body,
        out_shape=[
            pltpu.VMEM((width // NEAR, blocks * rows), F32),
            *[pltpu.VMEM((width // NEAR, (blocks + 1) * rows), F32)] * (NEAR - 1),
            pltpu.VMEM(resident.shape, BF16),
        ],
        in_specs=[vmem] * (3 + len(held)),
        out_specs=[vmem] * (NEAR + 1),
        input_output_aliases={2 + len(held): NEAR},
        scratch_shapes=[
            pltpu.VMEM((blocks * rows, 128), F32),
            pltpu.VMEM((blocks, 128, rows), F32),
            pltpu.VMEM((turned.shape[1], blocks * rows), BF16),
            pltpu.VMEM((blocks * 2 * width, 2 * rows), F32),
            pltpu.VMEM((blocks, width, rows), F32),
            pltpu.VMEM((blocks, width, rows), F32),
        ],
        compiler_params=pltpu.CompilerParams(vmem_limit_bytes=24 << 20),
        name="adjoint",
    )(turned, variance, *[in_vmem(array) for array in held], resident)


def combine_body(mine, *refs, count, final):
    got, outs = refs[:count], refs[count:]
    block, columns = mine.shape
    gains = [jnp.exp2(ref[:, columns:] - TOP) for ref in got]
    most = jnp.zeros((8, 128), F32)
    for at in range(0, columns, 128):
        span = slice(at, at + 128)
        total = mine[:, span]
        for ref, gain in zip(got, gains):
            total = total + ref[:, span] * gain
        outs[0][:, span] = total.astype(outs[0].dtype)
        if not final:
            for first in range(0, block, 8):
                most = jnp.maximum(most, jnp.abs(total[first : first + 8]))
    if not final:
        power, gain = scaling(most)
        outs[1][:, :columns] = outs[0][...] * gain
        outs[1][:, columns:] = jnp.broadcast_to(power, (block, 128))


def combine(mine, got, final):
    vmem = pl.BlockSpec(memory_space=pltpu.VMEM)
    if final:
        outs = [pltpu.VMEM(mine.shape, BF16)]
    else:
        outs = [pltpu.VMEM(mine.shape, F32), pltpu.VMEM(got[0].shape, F32)]
    return pl.pallas_call(
        functools.partial(combine_body, count=len(got), final=final),
        out_shape=outs,
        in_specs=[vmem] * (1 + len(got)),
        out_specs=[vmem] * len(outs),
        compiler_params=pltpu.CompilerParams(vmem_limit_bytes=24 << 20),
        name="combine",
    )(mine, *[in_vmem(array) for array in got])


def merge(first, second, step, sub):
    mine = (sub & step) == 0
    return jnp.where(mine, first, second) + pltpu.roll(jnp.where(mine, second, first), step, 0)


def forward_body(
    kernel,
    params0,
    params1,
    params2,
    params3,
    own,
    across,
    beside,
    params,
    weights,
    product,
    held,
    result,
    tall,
):
    sensors, length, width = kernel.shape
    probes, part = own.shape[0], own.shape[1]
    blocks = length // STEP
    rows = weights.shape[2]
    half = rows // 2
    block = params0.shape[0]
    near = lax.axis_index("srow") % NEAR
    for offset, piece in enumerate((params0, params1, params2, params3)):
        params[pl.ds(pl.multiple_of((near ^ offset) * block, block), block), :] = piece[...]
    for d in range(blocks):
        here = params[:, d * rows : (d + 1) * rows]
        weights[d, :width, :] = here
        if d == 0:
            before = jnp.zeros((width, half), BF16)
        else:
            before = params[:, d * rows - half : d * rows]
        weights[d, width:, :] = jnp.concatenate([before, here[:, :half]], axis=1)
    lane = lax.broadcasted_iota(jnp.int32, (8, 128), 1)
    sub = lax.broadcasted_iota(jnp.int32, (8, 128), 0)
    sets = causal_sets(blocks)

    def multiply(at, first, last):
        members = sets[at]
        acc = None
        for j in range(members[-1] + 1):
            left = jnp.concatenate(
                [
                    kernel[first:last, STEP * j + LAG * e : STEP * j + LAG * (e + 1), :].reshape(
                        (last - first) * LAG, width
                    )
                    for e in range(2)
                ],
                axis=1,
            )
            right = jnp.concatenate(
                [
                    weights[o - j] if o >= j else jnp.zeros((2 * width, rows), BF16)
                    for o in members
                ],
                axis=1,
            )
            step = jnp.dot(left, right, preferred_element_type=F32)
            acc = step if acc is None else acc + step
        product[at, first * LAG : last * LAG, : len(members) * rows] = acc

    def skew(at, group):
        for place, o in enumerate(sets[at]):
            summed = []
            for s in range(group * SENSORS, (group + 1) * SENSORS):
                if s >= sensors:
                    summed.append(jnp.zeros((8, 128), F32))
                    continue
                value = None
                for h in range(2):
                    first = s * LAG + 8 * h
                    shifted = pltpu.roll(
                        product[at, first : first + 8, place * rows : (place + 1) * rows],
                        8 * h * probes,
                        1,
                        stride=probes,
                        stride_axis=0,
                    )
                    inside = lane >= (sub + 8 * h) * probes
                    before = held[first : first + 8, :] if o > 0 else jnp.zeros_like(shifted)
                    mixed = jnp.where(inside, shifted, before)
                    if o + 1 < blocks:
                        held[first : first + 8, :] = shifted
                    value = mixed if value is None else value + mixed
                summed.append(value)
            step = 1
            while len(summed) > 1:
                summed = [
                    merge(summed[k], summed[k + 1], step, sub) for k in range(0, len(summed), 2)
                ]
                step *= 2
            result[o, group * SENSORS : (group + 1) * SENSORS, :] = summed[0]

    groups = range(-(-sensors // SENSORS))
    pieces = -(-sensors // 40)
    piece = -(-len(groups) // pieces)
    for at in range(len(sets) + 1):
        for first in range(0, len(groups), piece):
            if at < len(sets):
                multiply(at, first * SENSORS, min((first + piece) * SENSORS, sensors))
            if at > 0:
                for group in groups[first : first + piece]:
                    skew(at - 1, group)
    for o in range(blocks):
        tall[o * rows : (o + 1) * rows, :] = result[o].T
    me = lax.axis_index("pgrp")
    for offset, to in ((0, own), (2, across), (1, beside.at[0]), (3, beside.at[1])):
        first = (me ^ offset) * (part * probes)
        for n in range(probes):
            share = tall[pl.ds(first + n, part, stride=probes), :]
            to[n] = share[:, :sensors].astype(to.dtype)


def forward(params, kernel, shape):
    sensors, length, width = kernel.shape
    probes = shape[0]
    rows = probes * STEP
    blocks = length // STEP
    vmem = pl.BlockSpec(memory_space=pltpu.VMEM)
    return pl.pallas_call(
        forward_body,
        out_shape=[
            pltpu.VMEM(shape, F32),
            pltpu.VMEM(shape, F32),
            pltpu.VMEM((2,) + shape, BF16),
        ],
        in_specs=[vmem] * (1 + NEAR),
        out_specs=[vmem] * 3,
        scratch_shapes=[
            pltpu.VMEM((width, blocks * rows), BF16),
            pltpu.VMEM((blocks, 2 * width, rows), BF16),
            pltpu.VMEM((blocks // 2 + 1, sensors * LAG, 2 * rows), F32),
            pltpu.VMEM((sensors * LAG, rows), F32),
            pltpu.VMEM((blocks, 128, rows), F32),
            pltpu.VMEM((blocks * rows, 128), F32),
        ],
        compiler_params=pltpu.CompilerParams(vmem_limit_bytes=24 << 20),
        name="forward",
    )(kernel, *[in_vmem(array) for array in params])


def swap(array, axis, size, offset):
    return lax.ppermute(array, axis, [(i, i ^ offset) for i in range(size)])


def swap_sums(array, size, offset):
    return swap(array.astype(jnp.float16), "srow", size, offset).astype(F32)


def on_device(kernel, probes, prior_var, noise_var, *, parts, peers):
    series = probes.transpose(0, 2, 1)
    others = [swap(series, "pgrp", parts, offset) for offset in range(1, parts)]
    resident, turned, own, variance = prepare(kernel, series, prior_var)
    mine, *sent, resident = adjoint(turned, variance, [own] + others, resident)
    got = [swap_sums(sent[offset - 1], peers, offset) for offset in range(1, NEAR)]
    offset = NEAR
    while offset < peers:
        mine, away = combine(mine, got, False)
        got = [swap_sums(away, peers, offset)]
        offset *= 2
    (params,) = combine(mine, got, True)
    params = [params] + [swap(params, "srow", peers, offset) for offset in range(1, NEAR)]
    own, across, beside = forward(params, resident, series.shape)
    beside = swap(beside, "pgrp", parts, 1).astype(F32)
    across = swap((across + beside[1]).astype(BF16), "pgrp", parts, 2)
    total = own + beside[0] + across.astype(F32)
    total = total + noise_var[None, None, :] * series.astype(F32)
    return total.transpose(0, 2, 1)


def solution(mesh):
    placed = (P("srow", None, "pgrp"), P(None, "srow", "pgrp"), P("pgrp"), P("srow"))
    parts, peers = mesh.shape["pgrp"], mesh.shape["srow"]
    if parts != 4 or peers < NEAR or peers & (peers - 1):
        raise ValueError("unsupported mesh")
    body = functools.partial(on_device, parts=parts, peers=peers)
    return jax.shard_map(
        body, mesh=mesh, in_specs=placed, out_specs=P(None, "srow", "pgrp"), check_vma=False
    )
```

```python
import functools

import jax
import jax.numpy as jnp
from jax import lax
from jax.experimental import pallas as pl
from jax.experimental.pallas import tpu as pltpu
from jax.sharding import PartitionSpec as P

LAG = 16
STEP = 2 * LAG
SENSORS = 8
NEAR = 4
TOP = 13.0
F32 = jnp.float32
BF16 = jnp.bfloat16


def in_vmem(array):
    return pltpu.with_memory_space_constraint(array, pltpu.VMEM)


def causal_sets(blocks):
    sets = [(o - 1, o) for o in range(blocks - 1, 0, -2)][::-1]
    return [(0,)] + sets if blocks % 2 else sets


def sensor_groups(sensors):
    return [
        (first, min(first + SENSORS, sensors)) for first in range(0, sensors, SENSORS)
    ]


def scaling(peak):
    power = jnp.floor(jnp.log2(jnp.maximum(peak, 2.0**-100)))
    return power, jnp.exp2(TOP - power)


def prepare_body(
    kernel_hbm, own_hbm, prior, kernel, turned, own, variance, bound, sems
):
    sensors, length, width = kernel.shape
    block = width // NEAR
    near = lax.axis_index("srow") % NEAR
    groups = sensor_groups(sensors)
    series = pltpu.make_async_copy(own_hbm, own, sems.at[len(groups)])
    series.start()
    copies = []
    for at, (first, last) in enumerate(groups):
        span = pl.ds(first, last - first)
        copies.append(pltpu.make_async_copy(kernel_hbm.at[span], kernel.at[span], sems.at[at]))
    for copy in copies:
        copy.start()
    flipped = jnp.broadcast_to(prior[...], (width, width)).T
    for b in range(NEAR):
        variance[near ^ b] = flipped[b * block : (b + 1) * block]
    most = jnp.zeros((LAG, width), BF16)
    for at, (first, last) in enumerate(groups):
        copies[at].wait()
        for a in range(length // LAG):
            tile = kernel[first:last, a * LAG : (a + 1) * LAG, :]
            for s in range(last - first):
                most = jnp.maximum(most, jnp.abs(tile[s]))
            tile = tile.reshape(-1, width)
            if last - first < SENSORS:
                fill = jnp.zeros(((SENSORS - last + first) * LAG, width), BF16)
                tile = jnp.concatenate([tile, fill], axis=0)
            flipped = tile.T
            for b in range(NEAR):
                turned[
                    a // 2, NEAR - 1 - (near ^ b), a % 2, :, at * 128 : (at + 1) * 128
                ] = flipped[b * block : (b + 1) * block]
    spare = turned.shape[-1] - len(groups) * 128
    if spare:
        turned[..., len(groups) * 128 :] = jnp.zeros(turned.shape[:-1] + (spare,), BF16)
    peak = jnp.max(most.astype(F32), axis=(0, 1), keepdims=True)
    peak = peak * jnp.max(jnp.abs(prior[...]), axis=(0, 1), keepdims=True)
    bound[...] = jnp.broadcast_to(peak * float(sensors * length), bound.shape)
    series.wait()


def prepare(kernel, series, prior_var):
    sensors, length, width = kernel.shape
    lanes = 256 * -(-sensors // (2 * SENSORS))
    vmem = pl.BlockSpec(memory_space=pltpu.VMEM)
    hbm = pl.BlockSpec(memory_space=pltpu.HBM)
    return pl.pallas_call(
        prepare_body,
        out_shape=[
            pltpu.VMEM(kernel.shape, BF16),
            pltpu.VMEM((length // STEP, NEAR, 2, width // NEAR, lanes), BF16),
            pltpu.VMEM(series.shape, BF16),
            pltpu.VMEM((NEAR, width // NEAR, width), F32),
            pltpu.VMEM((8, 128), F32),
        ],
        in_specs=[hbm, hbm, vmem],
        out_specs=[vmem] * 5,
        scratch_shapes=[pltpu.SemaphoreType.DMA((len(sensor_groups(sensors)) + 1,))],
        compiler_params=pltpu.CompilerParams(vmem_limit_bytes=105 << 19),
        name="prepare",
    )(kernel, series, prior_var.reshape(1, width))


def expand_series(held, right, tall, series):
    probes, part, sensors = held[0].shape
    rows = probes * STEP
    blocks = tall.shape[0] // rows
    me = lax.axis_index("pgrp")
    most = None
    for offset, ref in enumerate(held):
        first = (me ^ offset) * (part * probes)
        for n in range(probes):
            value = ref[n].astype(F32)
            tall[pl.ds(first + n, part, stride=probes), :sensors] = value
            value = jnp.abs(value)
            most = value if most is None else jnp.maximum(most, value)
    for o in range(blocks):
        series[o] = tall[o * rows : (o + 1) * rows, :].astype(BF16).T.astype(F32)
    lane = lax.broadcasted_iota(jnp.int32, (8, 128), 1)
    sub = lax.broadcasted_iota(jnp.int32, (8, 128), 0)
    padded = right.shape[0] // LAG
    if padded > sensors:
        right[sensors * LAG :, :] = jnp.zeros(((padded - sensors) * LAG, right.shape[1]), BF16)

    def expand(s, first, last):
        tiles = {}
        for half in range(2):
            shift = (sub + 8 * half) * probes
            index = (lane + shift) % 128
            inside = lane + shift < 128
            held = None
            for o in range(first, min(last + 2, blocks)):
                row = series[o, pl.ds(s, 8, stride=0), :]
                moved = jnp.take_along_axis(row, index, axis=1, mode="promise_in_bounds")
                if held is not None:
                    tiles[o - 1, half] = jnp.where(inside, held, moved)
                held = moved
            if last + 1 == blocks:
                tiles[last, half] = jnp.where(inside, held, 0.0)
        for o in range(first, last + 1):
            right[s * LAG : (s + 1) * LAG, o * rows : (o + 1) * rows] = jnp.concatenate(
                [tiles[o, 0], tiles[o, 1]], axis=0
            ).astype(BF16)

    def run(members):
        for s in range(sensors):
            expand(s, members[0], members[-1])

    return run, jnp.max(most, axis=(0, 1), keepdims=True)


def adjoint_sums(turned, slots, right, product, even, odd, before_set):
    blocks, _, parities, block, lanes = turned.shape
    step_rows = len(slots) * parities * block
    per = max(1, 896 // step_rows)
    rows = even.shape[2]
    for members in causal_sets(blocks):
        before_set(members)
        columns = slice(members[0] * rows, (members[-1] + 1) * rows)
        for first in range(0, members[-1] + 1, per):
            last = min(first + per, members[-1] + 1)
            left = turned[first:last, slots[0] : slots[-1] + 1].reshape(-1, lanes)
            product[first * step_rows : last * step_rows, : len(members) * rows] = jnp.dot(
                left, right[:, columns], preferred_element_type=F32
            )
        for place, o in enumerate(members):
            for j in range(o + 1):
                for i in range(len(slots)):
                    for e, sums in enumerate((even, odd)):
                        at = j * step_rows + (i * parities + e) * block
                        value = product[at : at + block, place * rows : (place + 1) * rows]
                        span = slice(i * block, (i + 1) * block)
                        if j == 0:
                            sums[o, span, :] = value
                        else:
                            sums[o - j, span, :] += value


def write_sums(outs, slots, variance, even, odd, gain):
    blocks, _, rows = even.shape
    block = variance.shape[1]
    lane = lax.broadcasted_iota(jnp.int32, (8, 128), 1)
    first_half = lane < rows // 2
    for i, (out, slot) in enumerate(zip(outs, slots)):
        for first in range(0, block, 8):
            span = slice(i * block + first, i * block + first + 8)
            scale = variance[NEAR - 1 - slot, first : first + 8, :] * gain
            after = None
            for o in range(blocks - 1, -1, -1):
                moved = pltpu.roll(odd[o, span, :], rows // 2, 1)
                late = jnp.where(first_half, moved, 0.0 if after is None else after)
                after = moved
                out[o * block + first : o * block + first + 8, :] = (
                    even[o, span, :] + late
                ) * scale


def adjoint_away_body(turned, variance, bound, *refs):
    held, (to3, to2, to1, own_power, right) = refs[:NEAR], refs[NEAR : NEAR + 5]
    tall, series, product, even, odd = refs[NEAR + 5 :]
    run, most = expand_series(held, right, tall, series)
    power, gain = scaling(bound[...] * most)
    slots = list(range(NEAR - 1))
    adjoint_sums(turned, slots, right, product, even, odd, run)
    write_sums((to3, to2, to1), slots, variance, even, odd, gain)
    own_power[...] = power
    for to in (to3, to2, to1):
        to[-8:, :] = power


def adjoint_near_body(turned, variance, right, resident, mine, kept, product, even, odd):
    slots = [NEAR - 1]
    adjoint_sums(turned, slots, right, product, even, odd, lambda members: None)
    write_sums((mine,), slots, variance, even, odd, 1.0)


def adjoint(turned, variance, bound, held, resident):
    blocks, _, parities, block, lanes = turned.shape
    probes, part, sensors = held[0].shape
    rows = probes * STEP
    vmem = pl.BlockSpec(memory_space=pltpu.VMEM)
    params = pltpu.CompilerParams(
        vmem_limit_bytes=24 << 20
    )
    sent = pltpu.VMEM((blocks * block + 8, rows), F32)

    def sums(slots):
        return [
            pltpu.VMEM((blocks * slots * parities * block, 2 * rows), F32),
            pltpu.VMEM((blocks, slots * block, rows), F32),
            pltpu.VMEM((blocks, slots * block, rows), F32),
        ]

    to3, to2, to1, power, right = pl.pallas_call(
        adjoint_away_body,
        out_shape=[sent] * 3
        + [pltpu.VMEM((8, 128), F32), pltpu.VMEM((lanes, blocks * rows), BF16)],
        in_specs=[vmem] * (3 + len(held)),
        out_specs=[vmem] * 5,
        scratch_shapes=[
            pltpu.VMEM((blocks * rows, 128), F32),
            pltpu.VMEM((blocks, 128, rows), F32),
        ]
        + sums(NEAR - 1),
        compiler_params=params,
        name="adjoint_away",
    )(turned, variance, bound, *[in_vmem(array) for array in held])
    mine, resident = pl.pallas_call(
        adjoint_near_body,
        out_shape=[
            pltpu.VMEM((blocks * block, rows), F32),
            pltpu.VMEM(resident.shape, BF16),
        ],
        in_specs=[vmem] * 4,
        out_specs=[vmem] * 2,
        scratch_shapes=sums(1),
        input_output_aliases={3: 1},
        compiler_params=params,
        name="adjoint_near",
    )(turned, variance, right, resident)
    return mine, (to1, to2, to3), power, resident


def combine_body(mine, power, *refs, count, final):
    got, outs = refs[:count], refs[count:]
    size = mine.shape[0]
    gains = [jnp.exp2(ref[size:, :] - TOP) for ref in got]
    if not final:
        most = power[...]
        for ref in got:
            most = jnp.maximum(most, ref[size:, :])
        most = most + 2.0
        gain = jnp.exp2(TOP - most)
        outs[1][size:, :] = most
        outs[2][...] = most
    for first in range(0, size, LAG):
        span = slice(first, first + LAG)
        total = mine[span, :]
        for ref, factor in zip(got, gains):
            total = total + ref[span, :] * factor[:1, :]
        outs[0][span, :] = total.astype(outs[0].dtype)
        if not final:
            outs[1][span, :] = total * gain[:1, :]


def combine(mine, power, got, final):
    vmem = pl.BlockSpec(memory_space=pltpu.VMEM)
    outs = [pltpu.VMEM(mine.shape, BF16 if final else F32)]
    if not final:
        outs += [pltpu.VMEM(got[0].shape, F32), pltpu.VMEM(power.shape, F32)]
    return pl.pallas_call(
        functools.partial(combine_body, count=len(got), final=final),
        out_shape=outs,
        in_specs=[vmem] * (2 + len(got)),
        out_specs=[vmem] * len(outs),
        compiler_params=pltpu.CompilerParams(vmem_limit_bytes=24 << 20),
        name="combine",
    )(mine, power, *[in_vmem(array) for array in got])


def merge(first, second, step, sub):
    mine = (sub & step) == 0
    return jnp.where(mine, first, second) + pltpu.roll(jnp.where(mine, second, first), step, 0)


def forward_body(
    kernel,
    params0,
    params1,
    params2,
    params3,
    own,
    across,
    beside,
    params,
    weights,
    product,
    held,
    result,
    tall,
):
    sensors, length, width = kernel.shape
    probes, part = own.shape[0], own.shape[1]
    blocks = length // STEP
    rows = weights.shape[2]
    half = rows // 2
    block = width // NEAR
    near = lax.axis_index("srow") % NEAR
    for offset, piece in enumerate((params0, params1, params2, params3)):
        first = pl.multiple_of((near ^ offset) * block, block)
        for d in range(blocks):
            params[d, pl.ds(first, block), :] = piece[d * block : (d + 1) * block, :]
    for d in range(blocks):
        here = params[d]
        weights[d, :width, :] = here
        if d == 0:
            before = jnp.zeros((width, half), BF16)
        else:
            before = params[d - 1, :, half:]
        weights[d, width:, :] = jnp.concatenate([before, here[:, :half]], axis=1)
    lane = lax.broadcasted_iota(jnp.int32, (8, 128), 1)
    sub = lax.broadcasted_iota(jnp.int32, (8, 128), 0)
    sets = causal_sets(blocks)

    def multiply(at, first, last):
        members = sets[at]
        acc = None
        for j in range(members[-1] + 1):
            left = jnp.concatenate(
                [
                    kernel[first:last, STEP * j + LAG * e : STEP * j + LAG * (e + 1), :].reshape(
                        (last - first) * LAG, width
                    )
                    for e in range(2)
                ],
                axis=1,
            )
            right = jnp.concatenate(
                [
                    weights[o - j] if o >= j else jnp.zeros((2 * width, rows), BF16)
                    for o in members
                ],
                axis=1,
            )
            step = jnp.dot(left, right, preferred_element_type=F32)
            acc = step if acc is None else acc + step
        product[at, first * LAG : last * LAG, : len(members) * rows] = acc

    def skew(at, group):
        for place, o in enumerate(sets[at]):
            summed = []
            for s in range(group * SENSORS, (group + 1) * SENSORS):
                if s >= sensors:
                    summed.append(jnp.zeros((8, 128), F32))
                    continue
                value = None
                for h in range(2):
                    first = s * LAG + 8 * h
                    shifted = pltpu.roll(
                        product[at, first : first + 8, place * rows : (place + 1) * rows],
                        8 * h * probes,
                        1,
                        stride=probes,
                        stride_axis=0,
                    )
                    inside = lane >= (sub + 8 * h) * probes
                    before = held[first : first + 8, :] if o > 0 else jnp.zeros_like(shifted)
                    mixed = jnp.where(inside, shifted, before)
                    if o + 1 < blocks:
                        held[first : first + 8, :] = shifted
                    value = mixed if value is None else value + mixed
                summed.append(value)
            step = 1
            while len(summed) > 1:
                summed = [
                    merge(summed[k], summed[k + 1], step, sub) for k in range(0, len(summed), 2)
                ]
                step *= 2
            result[o, group * SENSORS : (group + 1) * SENSORS, :] = summed[0]

    groups = range(-(-sensors // SENSORS))
    pieces = -(-sensors // 40)
    piece = -(-len(groups) // pieces)
    for at in range(len(sets) + 1):
        for first in range(0, len(groups), piece):
            if at < len(sets):
                multiply(at, first * SENSORS, min((first + piece) * SENSORS, sensors))
            if at > 0:
                for group in groups[first : first + piece]:
                    skew(at - 1, group)
    for o in range(blocks):
        tall[o * rows : (o + 1) * rows, :] = result[o].T
    me = lax.axis_index("pgrp")
    for offset, to in ((0, own), (2, across), (1, beside.at[0]), (3, beside.at[1])):
        first = (me ^ offset) * (part * probes)
        for n in range(probes):
            share = tall[pl.ds(first + n, part, stride=probes), :]
            to[n] = share[:, :sensors].astype(to.dtype)


def forward(params, kernel, shape):
    sensors, length, width = kernel.shape
    probes = shape[0]
    rows = probes * STEP
    blocks = length // STEP
    vmem = pl.BlockSpec(memory_space=pltpu.VMEM)
    return pl.pallas_call(
        forward_body,
        out_shape=[
            pltpu.VMEM(shape, F32),
            pltpu.VMEM(shape, F32),
            pltpu.VMEM((2,) + shape, BF16),
        ],
        in_specs=[vmem] * (1 + NEAR),
        out_specs=[vmem] * 3,
        scratch_shapes=[
            pltpu.VMEM((blocks, width, rows), BF16),
            pltpu.VMEM((blocks, 2 * width, rows), BF16),
            pltpu.VMEM((blocks // 2 + 1, sensors * LAG, 2 * rows), F32),
            pltpu.VMEM((sensors * LAG, rows), F32),
            pltpu.VMEM((blocks, 128, rows), F32),
            pltpu.VMEM((blocks * rows, 128), F32),
        ],
        compiler_params=pltpu.CompilerParams(
            vmem_limit_bytes=24 << 20
        ),
        name="forward",
    )(kernel, *[in_vmem(array) for array in params])


def swap(array, axis, size, offset):
    return lax.ppermute(array, axis, [(i, i ^ offset) for i in range(size)])


def swap_sums(array, size, offset):
    return swap(array.astype(jnp.float16), "srow", size, offset).astype(F32)


def on_device(kernel, probes, prior_var, noise_var, *, parts, peers):
    series = probes.transpose(0, 2, 1)
    others = [swap(series, "pgrp", parts, offset) for offset in range(1, parts)]
    resident, turned, own, variance, bound = prepare(kernel, series, prior_var)
    mine, sent, power, resident = adjoint(turned, variance, bound, [own] + others, resident)
    got = [swap_sums(sent[offset - 1], peers, offset) for offset in range(1, NEAR)]
    offset = NEAR
    while offset < peers:
        mine, away, power = combine(mine, power, got, False)
        got = [swap_sums(away, peers, offset)]
        offset *= 2
    (params,) = combine(mine, power, got, True)
    params = [params] + [swap(params, "srow", peers, offset) for offset in range(1, NEAR)]
    own, across, beside = forward(params, resident, series.shape)
    beside = swap(beside, "pgrp", parts, 1).astype(F32)
    across = swap((across + beside[1]).astype(BF16), "pgrp", parts, 2)
    total = own + beside[0] + across.astype(F32)
    total = total + noise_var[None, None, :] * series.astype(F32)
    return total.transpose(0, 2, 1)


def solution(mesh):
    placed = (P("srow", None, "pgrp"), P(None, "srow", "pgrp"), P("pgrp"), P("srow"))
    parts, peers = mesh.shape["pgrp"], mesh.shape["srow"]
    if parts != 4 or peers < NEAR or peers & (peers - 1):
        raise ValueError("unsupported mesh")
    body = functools.partial(on_device, parts=parts, peers=peers)
    return jax.shard_map(
        body, mesh=mesh, in_specs=placed, out_specs=P(None, "srow", "pgrp"), check_vma=False
    )
```

```python
import functools

import jax
import jax.numpy as jnp
from jax import lax
from jax.experimental import pallas as pl
from jax.experimental.pallas import tpu as pltpu
from jax.sharding import PartitionSpec as P

LAG = 16
STEP = 2 * LAG
SENSORS = 8
NEAR = 4
TOP = 13.0
F32 = jnp.float32
BF16 = jnp.bfloat16


def in_vmem(array):
    return pltpu.with_memory_space_constraint(array, pltpu.VMEM)


def causal_sets(blocks):
    sets = [(o - 1, o) for o in range(blocks - 1, 0, -2)][::-1]
    return [(0,)] + sets if blocks % 2 else sets


def sensor_groups(sensors):
    return [
        (first, min(first + SENSORS, sensors)) for first in range(0, sensors, SENSORS)
    ]


def scaling(peak):
    power = jnp.floor(jnp.log2(jnp.maximum(peak, 2.0**-100)))
    return power, jnp.exp2(TOP - power)


def prepare_body(
    kernel_hbm, own_hbm, prior, kernel, turned, own, variance, bound, sems
):
    sensors, length, width = kernel.shape
    block = width // NEAR
    near = lax.axis_index("srow") % NEAR
    groups = sensor_groups(sensors)
    series = pltpu.make_async_copy(own_hbm, own, sems.at[len(groups)])
    series.start()
    copies = []
    for at, (first, last) in enumerate(groups):
        span = pl.ds(first, last - first)
        copies.append(pltpu.make_async_copy(kernel_hbm.at[span], kernel.at[span], sems.at[at]))
    for copy in copies:
        copy.start()
    flipped = jnp.broadcast_to(prior[...], (width, width)).T
    for b in range(NEAR):
        variance[near ^ b] = flipped[b * block : (b + 1) * block]
    most = jnp.zeros((LAG, width), BF16)
    for at, (first, last) in enumerate(groups):
        copies[at].wait()
        for a in range(length // LAG):
            tile = kernel[first:last, a * LAG : (a + 1) * LAG, :]
            for s in range(last - first):
                most = jnp.maximum(most, jnp.abs(tile[s]))
            tile = tile.reshape(-1, width)
            if last - first < SENSORS:
                fill = jnp.zeros(((SENSORS - last + first) * LAG, width), BF16)
                tile = jnp.concatenate([tile, fill], axis=0)
            flipped = tile.T
            for b in range(NEAR):
                turned[
                    a // 2, NEAR - 1 - (near ^ b), a % 2, :, at * 128 : (at + 1) * 128
                ] = flipped[b * block : (b + 1) * block]
    spare = turned.shape[-1] - len(groups) * 128
    if spare:
        turned[..., len(groups) * 128 :] = jnp.zeros(turned.shape[:-1] + (spare,), BF16)
    peak = jnp.max(most.astype(F32), axis=(0, 1), keepdims=True)
    peak = peak * jnp.max(jnp.abs(prior[...]), axis=(0, 1), keepdims=True)
    bound[...] = jnp.broadcast_to(peak * float(sensors * length), bound.shape)
    series.wait()


def prepare(kernel, series, prior_var):
    sensors, length, width = kernel.shape
    lanes = 256 * -(-sensors // (2 * SENSORS))
    vmem = pl.BlockSpec(memory_space=pltpu.VMEM)
    hbm = pl.BlockSpec(memory_space=pltpu.HBM)
    return pl.pallas_call(
        prepare_body,
        out_shape=[
            pltpu.VMEM(kernel.shape, BF16),
            pltpu.VMEM((length // STEP, NEAR, 2, width // NEAR, lanes), BF16),
            pltpu.VMEM(series.shape, BF16),
            pltpu.VMEM((NEAR, width // NEAR, width), F32),
            pltpu.VMEM((8, 128), F32),
        ],
        in_specs=[hbm, hbm, vmem],
        out_specs=[vmem] * 5,
        scratch_shapes=[pltpu.SemaphoreType.DMA((len(sensor_groups(sensors)) + 1,))],
        compiler_params=pltpu.CompilerParams(vmem_limit_bytes=105 << 19),
        name="prepare",
    )(kernel, series, prior_var.reshape(1, width))


def expand_series(held, right, tall, series):
    probes, part, sensors = held[0].shape
    rows = probes * STEP
    blocks = tall.shape[0] // rows
    me = lax.axis_index("pgrp")
    most = None
    for offset, ref in enumerate(held):
        first = (me ^ offset) * (part * probes)
        for n in range(probes):
            value = ref[n].astype(F32)
            tall[pl.ds(first + n, part, stride=probes), :sensors] = value
            value = jnp.abs(value)
            most = value if most is None else jnp.maximum(most, value)
    for o in range(blocks):
        series[o] = tall[o * rows : (o + 1) * rows, :].astype(BF16).T.astype(F32)
    lane = lax.broadcasted_iota(jnp.int32, (8, 128), 1)
    sub = lax.broadcasted_iota(jnp.int32, (8, 128), 0)
    padded = right.shape[0] // LAG
    if padded > sensors:
        right[sensors * LAG :, :] = jnp.zeros(((padded - sensors) * LAG, right.shape[1]), BF16)

    def expand(s, first, last):
        tiles = {}
        for half in range(2):
            shift = (sub + 8 * half) * probes
            index = (lane + shift) % 128
            inside = lane + shift < 128
            held = None
            for o in range(first, min(last + 2, blocks)):
                row = series[o, pl.ds(s, 8, stride=0), :]
                moved = jnp.take_along_axis(row, index, axis=1, mode="promise_in_bounds")
                if held is not None:
                    tiles[o - 1, half] = jnp.where(inside, held, moved)
                held = moved
            if last + 1 == blocks:
                tiles[last, half] = jnp.where(inside, held, 0.0)
        for o in range(first, last + 1):
            right[s * LAG : (s + 1) * LAG, o * rows : (o + 1) * rows] = jnp.concatenate(
                [tiles[o, 0], tiles[o, 1]], axis=0
            ).astype(BF16)

    def run(members):
        for s in range(sensors):
            expand(s, members[0], members[-1])

    return run, jnp.max(most, axis=(0, 1), keepdims=True)


def adjoint_sums(turned, slots, right, product, even, odd, before_set):
    blocks, _, parities, block, lanes = turned.shape
    step_rows = len(slots) * parities * block
    per = max(1, 896 // step_rows)
    rows = even.shape[2]
    for members in causal_sets(blocks):
        before_set(members)
        columns = slice(members[0] * rows, (members[-1] + 1) * rows)
        for first in range(0, members[-1] + 1, per):
            last = min(first + per, members[-1] + 1)
            left = turned[first:last, slots[0] : slots[-1] + 1].reshape(-1, lanes)
            product[first * step_rows : last * step_rows, : len(members) * rows] = jnp.dot(
                left, right[:, columns], preferred_element_type=F32
            )
        for place, o in enumerate(members):
            for j in range(o + 1):
                for i in range(len(slots)):
                    for e, sums in enumerate((even, odd)):
                        at = j * step_rows + (i * parities + e) * block
                        value = product[at : at + block, place * rows : (place + 1) * rows]
                        span = slice(i * block, (i + 1) * block)
                        if j == 0:
                            sums[o, span, :] = value
                        else:
                            sums[o - j, span, :] += value


def write_sums(outs, slots, variance, even, odd, gain):
    blocks, _, rows = even.shape
    block = variance.shape[1]
    lane = lax.broadcasted_iota(jnp.int32, (8, 128), 1)
    first_half = lane < rows // 2
    for i, (out, slot) in enumerate(zip(outs, slots)):
        for first in range(0, block, 8):
            span = slice(i * block + first, i * block + first + 8)
            scale = variance[NEAR - 1 - slot, first : first + 8, :] * gain
            after = None
            for o in range(blocks - 1, -1, -1):
                moved = pltpu.roll(odd[o, span, :], rows // 2, 1)
                late = jnp.where(first_half, moved, 0.0 if after is None else after)
                after = moved
                out[o * block + first : o * block + first + 8, :] = (
                    even[o, span, :] + late
                ) * scale


def adjoint_away_body(turned, variance, bound, *refs):
    held, (to3, to2, to1, own_power, right) = refs[:NEAR], refs[NEAR : NEAR + 5]
    tall, series, product, even, odd = refs[NEAR + 5 :]
    run, most = expand_series(held, right, tall, series)
    power, gain = scaling(bound[...] * most)
    slots = list(range(NEAR - 1))
    adjoint_sums(turned, slots, right, product, even, odd, run)
    write_sums((to3, to2, to1), slots, variance, even, odd, gain)
    own_power[...] = power
    for to in (to3, to2, to1):
        to[-8:, :] = power


def adjoint_near_body(turned, variance, right, resident, mine, kept, product, even, odd):
    slots = [NEAR - 1]
    adjoint_sums(turned, slots, right, product, even, odd, lambda members: None)
    write_sums((mine,), slots, variance, even, odd, 1.0)


def adjoint(turned, variance, bound, held, resident):
    blocks, _, parities, block, lanes = turned.shape
    probes, part, sensors = held[0].shape
    rows = probes * STEP
    vmem = pl.BlockSpec(memory_space=pltpu.VMEM)
    params = pltpu.CompilerParams(
        vmem_limit_bytes=24 << 20
    )
    sent = pltpu.VMEM((blocks * block + 8, rows), F32)

    def sums(slots):
        return [
            pltpu.VMEM((blocks * slots * parities * block, 2 * rows), F32),
            pltpu.VMEM((blocks, slots * block, rows), F32),
            pltpu.VMEM((blocks, slots * block, rows), F32),
        ]

    to3, to2, to1, power, right = pl.pallas_call(
        adjoint_away_body,
        out_shape=[sent] * 3
        + [pltpu.VMEM((8, 128), F32), pltpu.VMEM((lanes, blocks * rows), BF16)],
        in_specs=[vmem] * (3 + len(held)),
        out_specs=[vmem] * 5,
        scratch_shapes=[
            pltpu.VMEM((blocks * rows + 8, 128), F32),
            pltpu.VMEM((blocks, 128, rows), F32),
        ]
        + sums(NEAR - 1),
        compiler_params=params,
        name="adjoint_away",
    )(turned, variance, bound, *[in_vmem(array) for array in held])
    mine, resident = pl.pallas_call(
        adjoint_near_body,
        out_shape=[
            pltpu.VMEM((blocks * block, rows), F32),
            pltpu.VMEM(resident.shape, BF16),
        ],
        in_specs=[vmem] * 4,
        out_specs=[vmem] * 2,
        scratch_shapes=sums(1),
        input_output_aliases={3: 1},
        compiler_params=params,
        name="adjoint_near",
    )(turned, variance, right, resident)
    return mine, (to1, to2, to3), power, resident


def combine_body(mine, power, *refs, count, final):
    got, outs = refs[:count], refs[count:]
    size = mine.shape[0]
    gains = [jnp.exp2(ref[size:, :] - TOP) for ref in got]
    if not final:
        most = power[...]
        for ref in got:
            most = jnp.maximum(most, ref[size:, :])
        most = most + 2.0
        gain = jnp.exp2(TOP - most)
        outs[1][size:, :] = most
        outs[2][...] = most
    for first in range(0, size, LAG):
        span = slice(first, first + LAG)
        total = mine[span, :]
        for ref, factor in zip(got, gains):
            total = total + ref[span, :] * factor[:1, :]
        outs[0][span, :] = total.astype(outs[0].dtype)
        if not final:
            outs[1][span, :] = total * gain[:1, :]


def combine(mine, power, got, final):
    vmem = pl.BlockSpec(memory_space=pltpu.VMEM)
    outs = [pltpu.VMEM(mine.shape, BF16 if final else F32)]
    if not final:
        outs += [pltpu.VMEM(got[0].shape, F32), pltpu.VMEM(power.shape, F32)]
    return pl.pallas_call(
        functools.partial(combine_body, count=len(got), final=final),
        out_shape=outs,
        in_specs=[vmem] * (2 + len(got)),
        out_specs=[vmem] * len(outs),
        compiler_params=pltpu.CompilerParams(vmem_limit_bytes=24 << 20),
        name="combine",
    )(mine, power, *[in_vmem(array) for array in got])


def merge(first, second, step, sub):
    mine = (sub & step) == 0
    return jnp.where(mine, first, second) + pltpu.roll(jnp.where(mine, second, first), step, 0)


def forward_body(
    kernel,
    params0,
    params1,
    params2,
    params3,
    own,
    across,
    beside,
    params,
    weights,
    product,
    held,
    result,
    tall,
):
    sensors, length, width = kernel.shape
    probes, part = own.shape[0], own.shape[1]
    blocks = length // STEP
    rows = weights.shape[2]
    half = rows // 2
    block = width // NEAR
    near = lax.axis_index("srow") % NEAR
    for offset, piece in enumerate((params0, params1, params2, params3)):
        first = pl.multiple_of((near ^ offset) * block, block)
        for d in range(blocks):
            params[d, pl.ds(first, block), :] = piece[d * block : (d + 1) * block, :]
    for d in range(blocks):
        here = params[d]
        weights[d, :width, :] = here
        if d == 0:
            before = jnp.zeros((width, half), BF16)
        else:
            before = params[d - 1, :, half:]
        weights[d, width:, :] = jnp.concatenate([before, here[:, :half]], axis=1)
    lane = lax.broadcasted_iota(jnp.int32, (8, 128), 1)
    sub = lax.broadcasted_iota(jnp.int32, (8, 128), 0)
    sets = causal_sets(blocks)

    def multiply(at, first, last):
        members = sets[at]
        acc = None
        for j in range(members[-1] + 1):
            left = jnp.concatenate(
                [
                    kernel[first:last, STEP * j + LAG * e : STEP * j + LAG * (e + 1), :].reshape(
                        (last - first) * LAG, width
                    )
                    for e in range(2)
                ],
                axis=1,
            )
            right = jnp.concatenate(
                [
                    weights[o - j] if o >= j else jnp.zeros((2 * width, rows), BF16)
                    for o in members
                ],
                axis=1,
            )
            step = jnp.dot(left, right, preferred_element_type=F32)
            acc = step if acc is None else acc + step
        product[at, first * LAG : last * LAG, : len(members) * rows] = acc

    def skew(at, group):
        for place, o in enumerate(sets[at]):
            summed = []
            for s in range(group * SENSORS, (group + 1) * SENSORS):
                if s >= sensors:
                    summed.append(jnp.zeros((8, 128), F32))
                    continue
                value = None
                for h in range(2):
                    first = s * LAG + 8 * h
                    shifted = pltpu.roll(
                        product[at, first : first + 8, place * rows : (place + 1) * rows],
                        8 * h * probes,
                        1,
                        stride=probes,
                        stride_axis=0,
                    )
                    inside = lane >= (sub + 8 * h) * probes
                    before = held[first : first + 8, :] if o > 0 else jnp.zeros_like(shifted)
                    mixed = jnp.where(inside, shifted, before)
                    if o + 1 < blocks:
                        held[first : first + 8, :] = shifted
                    value = mixed if value is None else value + mixed
                summed.append(value)
            step = 1
            while len(summed) > 1:
                summed = [
                    merge(summed[k], summed[k + 1], step, sub) for k in range(0, len(summed), 2)
                ]
                step *= 2
            result[o, group * SENSORS : (group + 1) * SENSORS, :] = summed[0]

    groups = range(-(-sensors // SENSORS))
    pieces = -(-sensors // 40)
    piece = -(-len(groups) // pieces)
    for at in range(len(sets) + 1):
        for first in range(0, len(groups), piece):
            if at < len(sets):
                multiply(at, first * SENSORS, min((first + piece) * SENSORS, sensors))
            if at > 0:
                for group in groups[first : first + piece]:
                    skew(at - 1, group)
    for o in range(blocks):
        tall[o * rows : (o + 1) * rows, :] = result[o].T
    me = lax.axis_index("pgrp")
    for offset, to in ((0, own), (2, across), (1, beside.at[0]), (3, beside.at[1])):
        first = (me ^ offset) * (part * probes)
        for n in range(probes):
            share = tall[pl.ds(first + n, part, stride=probes), :]
            to[n] = share[:, :sensors].astype(to.dtype)


def forward(params, kernel, shape):
    sensors, length, width = kernel.shape
    probes = shape[0]
    rows = probes * STEP
    blocks = length // STEP
    vmem = pl.BlockSpec(memory_space=pltpu.VMEM)
    return pl.pallas_call(
        forward_body,
        out_shape=[
            pltpu.VMEM(shape, F32),
            pltpu.VMEM(shape, F32),
            pltpu.VMEM((2,) + shape, BF16),
        ],
        in_specs=[vmem] * (1 + NEAR),
        out_specs=[vmem] * 3,
        scratch_shapes=[
            pltpu.VMEM((blocks, width, rows), BF16),
            pltpu.VMEM((blocks, 2 * width, rows), BF16),
            pltpu.VMEM((blocks // 2 + 1, sensors * LAG, 2 * rows), F32),
            pltpu.VMEM((sensors * LAG, rows), F32),
            pltpu.VMEM((blocks, 128, rows), F32),
            pltpu.VMEM((blocks * rows + 8, 128), F32),
        ],
        compiler_params=pltpu.CompilerParams(
            vmem_limit_bytes=24 << 20
        ),
        name="forward",
    )(kernel, *[in_vmem(array) for array in params])


def swap(array, axis, size, offset):
    return lax.ppermute(array, axis, [(i, i ^ offset) for i in range(size)])


def swap_sums(array, size, offset):
    return swap(array.astype(jnp.float16), "srow", size, offset).astype(F32)


def on_device(kernel, probes, prior_var, noise_var, *, parts, peers):
    series = probes.transpose(0, 2, 1)
    others = [swap(series, "pgrp", parts, offset) for offset in range(1, parts)]
    resident, turned, own, variance, bound = prepare(kernel, series, prior_var)
    mine, sent, power, resident = adjoint(turned, variance, bound, [own] + others, resident)
    got = [swap_sums(sent[offset - 1], peers, offset) for offset in range(1, NEAR)]
    offset = NEAR
    while offset < peers:
        mine, away, power = combine(mine, power, got, False)
        got = [swap_sums(away, peers, offset)]
        offset *= 2
    (params,) = combine(mine, power, got, True)
    params = [params] + [swap(params, "srow", peers, offset) for offset in range(1, NEAR)]
    own, across, beside = forward(params, resident, series.shape)
    beside = swap(beside, "pgrp", parts, 1).astype(F32)
    across = swap((across + beside[1]).astype(BF16), "pgrp", parts, 2)
    total = own + beside[0] + across.astype(F32)
    total = total + noise_var[None, None, :] * series.astype(F32)
    return total.transpose(0, 2, 1)


def solution(mesh):
    placed = (P("srow", None, "pgrp"), P(None, "srow", "pgrp"), P("pgrp"), P("srow"))
    parts, peers = mesh.shape["pgrp"], mesh.shape["srow"]
    if parts != 4 or peers < NEAR or peers & (peers - 1):
        raise ValueError("unsupported mesh")
    body = functools.partial(on_device, parts=parts, peers=peers)
    return jax.shard_map(
        body, mesh=mesh, in_specs=placed, out_specs=P(None, "srow", "pgrp"), check_vma=False
    )
```
